256 devices in a mesh: pair: 16 (over z, core), red: 16 (over x, y).
Axes of the slice: x: 4, y: 4, z: 8, core: 2. Of those that a mesh axis runs over, the one named last changes fastest.
Arguments:
- three_center: bfloat16 [2304, 256, 256], P('pair', 'red'), may hold values from -0.375 to 0.375
- occ_src: int32 [256, 16], P('red'), may hold values from 0 to 15, as said below
- occ_block: int32 [256, 16], P('red'), may hold values from 0 to 31
- occ_blocks: bfloat16 [512, 256], P('red'), may hold values from -0.375 to 0.375
- virt_block: int32 [16, 16, 1], P('red'), may hold values from 0 to 31, as said below
- virt_blocks: bfloat16 [16, 32, 256], P('red', 'pair'), may hold values from -1.5 to 1.5
Outputs:
- chi: float32 [2304, 2304], P('pair', 'red')
The draws below stay inside these ranges and needn't reach their ends.
Inputs may be any that keep to these rules, and one draw needn't show every extreme that they name: `occ_src`: the 16 entries of a row are distinct. `virt_block`: every block listed for tile t of a red group lies from (t) * 2 to (t) * 2 + 1.
All inputs are finite; a program needn't handle non-finite values.
Results may differ from the reference program's by a relative error of at most 0.0041.
Values may be sent and summed in bfloat16 or wider, within the bound.
A program may use at most 128 MiB of HBM per device.

```python
import jax
import jax.numpy as jnp
from jax import lax

BLK = 16
NAUX = 2304
TPD = 1
NT = 16
NTT = 256
NS = 16
NOB = 32
NVB = 2
N_PAIR = 16
N_RED = 16


def draw_occ_src(key, part):
    keys = jax.random.split(key, NTT)
    orders = jax.vmap(lambda single: jax.random.permutation(single, NT))(keys)
    return orders[:, :NS].astype(jnp.int32)


def draw_virt_block(key, part):
    groups = NTT // NT
    base = jax.random.randint(key, (groups, NT, TPD), 0, NVB)
    base = base.at[:, 0, 0].set(0)
    base = base.at[:, NT - 1, TPD - 1].set(NVB - 1)
    offset = jnp.arange(NT, dtype=jnp.int32) // TPD * NVB
    return (base + offset[None, :, None]).astype(jnp.int32)


def touch_ends(array, stream_key, smallest, top_value):
    index_at = [jax.random.randint(jax.random.fold_in(stream_key, axis), (), 0, length) for axis, length in enumerate(array.shape)]
    widest = array.shape.index(max(array.shape))
    neighbour = index_at[:widest] + [(index_at[widest] + 1) % array.shape[widest]] + index_at[widest + 1:]
    return array.at[tuple(index_at)].set(smallest).at[tuple(neighbour)].set(top_value)


def level_of(stream_key, extent, shards, least, largest):
    def one(axis_at, parts):
        heights = jax.random.uniform(jax.random.fold_in(jax.random.fold_in(stream_key, 6), axis_at), (parts,), jnp.float32, least / len(shards), largest / len(shards))
        return jnp.repeat(jnp.exp(heights), extent[axis_at] // parts).reshape((-1,) + (1,) * (len(extent) - axis_at - 1))

    loudness = one(*shards[0])
    for cut in shards[1:]:
        loudness = loudness * one(*cut)
    return loudness


def gaussian(key, shape, spread, reach, shards=(), kind=jnp.bfloat16):
    drawn = spread * jax.random.normal(key, shape, jnp.float32)
    if shards:
        drawn = drawn * level_of(key, shape, shards, -0.22, 0.18)
    return jnp.clip(drawn, -reach, reach).astype(kind)


def setup_inputs(seed: int = 0) -> dict:
    seeds = jax.random.split(jax.random.key(seed), 7)
    return {
        "three_center": gaussian(seeds[0], (NAUX, NTT, BLK * BLK), 0.0625, 0.375, ((0, 16), (1, 16))),
        "occ_src": draw_occ_src(jax.random.fold_in(seeds[6], 71), 0),
        "occ_block": touch_ends(jax.random.randint(seeds[2], (NTT, NS), 0, NOB), jax.random.fold_in(seeds[2], 1), 0, NOB - 1).astype(jnp.int32),
        "occ_blocks": gaussian(seeds[3], (N_RED * NOB, BLK * BLK), (BLK * NS) ** -0.5, 0.375, ((0, 16),)),
        "virt_block": draw_virt_block(jax.random.fold_in(seeds[6], 71), 0),
        "virt_blocks": gaussian(seeds[5], (N_RED, N_PAIR * NVB, BLK * BLK), (BLK * TPD) ** -0.5, 1.5, ((0, 16), (1, 16))),
    }


def reference(three_center, occ_src, occ_block, occ_blocks, virt_block, virt_blocks):
    groups = jnp.arange(N_RED, dtype=jnp.int32)
    owner = (jnp.arange(NT, dtype=jnp.int32) // TPD) * TPD

    def one_group(total, group):
        tiles = lax.dynamic_slice_in_dim(three_center, group * NT, NT, 1)
        blocks = tiles.astype(jnp.float32).reshape(NAUX, NT, BLK, BLK)
        sources = lax.dynamic_slice_in_dim(occ_src, group * NT, NT, 0)
        chosen = lax.dynamic_slice_in_dim(occ_block, group * NT, NT, 0)
        density = lax.dynamic_slice_in_dim(occ_blocks, group * NOB, NOB, 0).astype(jnp.float32).reshape(NOB, BLK, BLK)
        half = jnp.zeros((NAUX, NT, BLK, BLK), jnp.float32)
        for slot in range(NS):
            half = half + jnp.einsum('tml,ptln->ptmn', density[chosen[:, slot]], blocks[:, sources[:, slot]])
        half = lax.optimization_barrier(half.astype(jnp.bfloat16)).astype(jnp.float32)
        virtual = virt_blocks[group].astype(jnp.float32).reshape(-1, BLK, BLK)
        listed = virt_block[group]
        kernel = jnp.zeros((NAUX, NT, BLK, BLK), jnp.float32)
        for column in range(TPD):
            kernel = kernel + jnp.einsum('ptml,tln->ptmn', half[:, owner + column], virtual[listed[:, column]])
        kernel = kernel.astype(jnp.bfloat16).reshape(NAUX, NT * BLK * BLK)
        flat = tiles.reshape(NAUX, NT * BLK * BLK)
        term = lax.dot_general(flat, kernel, (((1,), (1,)), ((), ())), preferred_element_type=jnp.float32)
        return total + term, None

    chi, unused = lax.scan(one_group, jnp.zeros((NAUX, NAUX), jnp.float32), groups)
    return chi
```

```python
import jax
import jax.numpy as jnp
from jax import lax
from jax.experimental import pallas as pl
from jax.experimental.pallas import tpu as pltpu
from jax.sharding import PartitionSpec as P

BLK = 16
MESH = pl.DeviceIdType.MESH
CHUNKS = 3
OFFSETS = (0, -1, 2, 3, 0, 1, -2, -3)
PAIRS = (
    (0, 0), (4, 0),
    (2, 0), (6, 0), (0, 2), (6, 2),
    (3, 0), (7, 0), (3, 2), (7, 2),
    (1, 0), (5, 0), (1, 2), (5, 2),
    (1, 3), (7, 3),
)


def mixing_matrix(occ_src, occ_block, occ_blocks):
    ntiles = occ_src.shape[0]
    nblocks = occ_blocks.shape[0]
    block_hot = (
        occ_block[:, :, None] == jnp.arange(nblocks, dtype=jnp.int32)[None, None, :]
    ).astype(jnp.bfloat16)
    picked = jnp.einsum(
        "tsb,bk->tsk", block_hot, occ_blocks, preferred_element_type=jnp.float32
    ).astype(jnp.bfloat16)
    source_hot = (occ_src[:, :, None] == jnp.arange(ntiles, dtype=jnp.int32)[None, None, :]).astype(
        jnp.bfloat16
    )
    mixing = jnp.einsum(
        "tsk,tsa->tka", source_hot, picked, preferred_element_type=jnp.float32
    ).astype(jnp.bfloat16)
    mixing = mixing.reshape(ntiles, ntiles, BLK, BLK)
    return mixing.transpose(1, 3, 0, 2).reshape(ntiles * BLK, ntiles * BLK)


def kernel(
    tiles_hbm, mix_ref, virt_ref, out_ref,
    rows, wide, xs, kv, virt, kern, sendbuf, recvbuf,
    far_send, far_recv, fwd_send, fwd_recv, near_send, near_recv,
    sib_send, sib_recv, virt_send, virt_recv, part_send, part_recv, local_sem,
):
    naux = tiles_hbm.shape[0]
    ntiles = 16
    area = 256
    step_rows = naux // CHUNKS
    me = lax.axis_index("pair")
    red = lax.axis_index("red")
    z, core = me // 2, me % 2
    sign = 1 - 2 * core

    def at(offset, which):
        return ((z + sign * offset + 16) % 8) * 2 + which

    col_z, col_core = red // 2, red % 2
    csign = 1 - 2 * col_core
    delta = (csign * (z - col_z) + 16) % 8
    same = core == col_core
    col_off_same = jnp.where(delta == 4, 3, jnp.where((delta == 5) | (delta == 6) | (delta == 1), 2, 0))
    col_off_other = jnp.where(delta == 2, 3, jnp.where((delta == 3) | (delta == 4) | (delta == 7), 2, 0))
    col_off = jnp.where(same, col_off_same, col_off_other)
    maker = ((col_z - csign * col_off + 16) % 8) * 2 + col_core

    barrier = pltpu.get_barrier_semaphore()

    def greet(o, c):
        pl.semaphore_signal(barrier, inc=1, device_id=((me + o) % 16, red), device_id_type=MESH)
        return c

    lax.fori_loop(1, 16, greet, 0)

    def greet_maker(g, c):
        own = (maker == me) & (g == red)

        @pl.when(jnp.logical_not(own))
        def _():
            pl.semaphore_signal(barrier, inc=1, device_id=(maker, g), device_id_type=MESH)

        return c

    lax.fori_loop(0, 16, greet_maker, 0)
    pl.semaphore_wait(barrier, 31 - jnp.where(maker == me, 1, 0))

    def slot(i):
        return rows.at[pl.ds(i * naux, naux), :]

    def piece(i, c):
        return rows.at[pl.ds(i * naux + c * step_rows, step_rows), :]

    far = []
    for c in range(CHUNKS):
        copy = pltpu.make_async_remote_copy(
            src_ref=tiles_hbm.at[pl.ds(c * step_rows, step_rows), :], dst_ref=piece(2, c),
            send_sem=far_send.at[c], recv_sem=far_recv.at[c],
            device_id=(at(-2, core), red), device_id_type=MESH,
        )
        copy.start()
        far.append(copy)
    own_copy = pltpu.make_async_copy(tiles_hbm, slot(0), local_sem.at[0])
    own_copy.start()
    own_virt = pltpu.make_async_copy(virt_ref, virt.at[me], local_sem.at[1])
    own_virt.start()

    def virt_copy(o):
        return pltpu.make_async_remote_copy(
            src_ref=virt_ref, dst_ref=virt.at[me],
            send_sem=virt_send.at[o], recv_sem=virt_recv.at[me],
            device_id=((me + o) % 16, red), device_id_type=MESH,
        )

    def virt_start(o, c):
        virt_copy(o).start()
        return c

    lax.fori_loop(1, 16, virt_start, 0)

    def sibling(i, src):
        return pltpu.make_async_remote_copy(
            src_ref=src, dst_ref=slot(4 + i),
            send_sem=sib_send.at[i], recv_sem=sib_recv.at[i],
            device_id=(z * 2 + 1 - core, red), device_id_type=MESH,
        )

    sib = [sibling(0, tiles_hbm)] + [sibling(i, slot(i)) for i in (1, 2, 3)]
    sib[0].start()
    near = pltpu.make_async_remote_copy(
        src_ref=tiles_hbm, dst_ref=slot(1), send_sem=near_send.at[0], recv_sem=near_recv.at[0],
        device_id=(at(1, core), red), device_id_type=MESH,
    )
    fwd = [
        pltpu.make_async_remote_copy(
            src_ref=piece(2, c), dst_ref=piece(3, c),
            send_sem=fwd_send.at[c], recv_sem=fwd_recv.at[c],
            device_id=(at(-1, core), red), device_id_type=MESH,
        )
        for c in range(CHUNKS)
    ]

    lane = lax.broadcasted_iota(jnp.int32, (BLK, area), 1)
    sub = lax.broadcasted_iota(jnp.int32, (BLK, area), 0)
    keep = (lane % BLK) == sub
    grow = lax.broadcasted_iota(jnp.int32, (area, area), 0)
    glane = lax.broadcasted_iota(jnp.int32, (area, area), 1)

    def widen(t, c):
        pick = (grow == t * BLK + glane // BLK).astype(jnp.float32).astype(jnp.bfloat16)
        xs[...] = jnp.dot(mix_ref[...], pick, preferred_element_type=jnp.float32)

        def group(q, c2):
            base = q * 16
            for r in range(16):
                row = xs[pl.ds(base + r, 1), :]
                value = jnp.where(keep, jnp.broadcast_to(row, (BLK, area)), 0.0)
                wide[t, pl.ds(pl.multiple_of((base + r) * BLK, BLK), BLK), :] = value.astype(jnp.bfloat16)
            return c2

        lax.fori_loop(0, area // 16, group, 0)
        return c

    lax.fori_loop(0, ntiles, widen, 0)

    own_virt.wait()

    def virt_wait(o, c):
        src = (me + o) % 16
        pltpu.make_async_remote_copy(
            src_ref=virt_ref, dst_ref=virt.at[src],
            send_sem=virt_send.at[o], recv_sem=virt_recv.at[src],
            device_id=(src, red), device_id_type=MESH,
        ).wait()
        return c

    lax.fori_loop(1, 16, virt_wait, 0)
    diagonal = (grow // BLK) == (glane // BLK)

    def spread(t, c):
        block = virt[t].astype(jnp.float32)
        tall = jnp.concatenate([block] * BLK, axis=0)
        kv[t] = jnp.where(diagonal, tall, 0.0).astype(jnp.bfloat16)
        return c

    lax.fori_loop(0, ntiles, spread, 0)

    def make_kernel(first, count, begin, end):
        def tile(t, c):
            half = jnp.dot(
                rows[first * naux:(first + count) * naux, :], wide[t], preferred_element_type=jnp.float32
            ).astype(jnp.bfloat16)
            value = jnp.dot(half, kv[t], preferred_element_type=jnp.float32).astype(jnp.bfloat16)
            k0 = {0: 0, 2: 1, 3: 2}[first]
            kern[k0 * naux:(k0 + count) * naux, pl.ds(pl.multiple_of(t * area, area), area)] = value
            return c

        lax.fori_loop(begin, end, tile, 0)

    def product(n):
        row_slot, col_slot = PAIRS[n]
        k0 = {0: 0, 2: 1, 3: 2}[col_slot]
        value = lax.dot_general(
            rows[row_slot * naux:(row_slot + 1) * naux, :], kern[k0 * naux:(k0 + 1) * naux, :],
            (((1,), (1,)), ((), ())), preferred_element_type=jnp.float32,
        )
        sendbuf[n] = value.astype(jnp.bfloat16)
        to_pair = at(OFFSETS[row_slot], core if row_slot < 4 else 1 - core)
        to_red = at(OFFSETS[col_slot], core)
        own = (to_pair == me) & (to_red == red)

        @pl.when(own)
        def _():
            pltpu.make_async_copy(sendbuf.at[n], recvbuf.at[red], part_recv.at[red]).start()

        @pl.when(jnp.logical_not(own))
        def _():
            pltpu.make_async_remote_copy(
                src_ref=sendbuf.at[n], dst_ref=recvbuf.at[red],
                send_sem=part_send.at[n], recv_sem=part_recv.at[red],
                device_id=(to_pair, to_red), device_id_type=MESH,
            ).start()

    own_copy.wait()

    def relay(c):
        far[c].wait_recv()
        fwd[c].start()

    relay(0)
    make_kernel(0, 1, 0, 8)
    relay(1)
    near.start()
    make_kernel(0, 1, 8, 16)
    relay(2)
    sib[2].start()
    sib[0].wait_recv()
    product(0)
    product(1)
    make_kernel(2, 1, 0, 16)
    sib[2].wait_recv()
    for n in range(2, 6):
        product(n)
    for c in range(CHUNKS):
        fwd[c].wait_recv()
    sib[3].start()
    near.wait_recv()
    sib[1].start()
    make_kernel(3, 1, 0, 16)
    sib[3].wait_recv()
    sib[1].wait_recv()
    for n in range(6, 16):
        product(n)

    total = jnp.zeros((naux, naux), jnp.float32)
    for g in range(16):
        pltpu.make_async_copy(sendbuf.at[0], recvbuf.at[g], part_recv.at[g]).wait()
    for g in range(16):
        total = total + recvbuf[g].astype(jnp.float32)
    out_ref[...] = total

    for c in range(CHUNKS):
        far[c].wait_send()
        fwd[c].wait_send()
    near.wait_send()
    for copy in sib:
        copy.wait_send()
    for n in range(16):
        row_slot, col_slot = PAIRS[n]
        to_pair = at(OFFSETS[row_slot], core if row_slot < 4 else 1 - core)
        to_red = at(OFFSETS[col_slot], core)
        own = (to_pair == me) & (to_red == red)

        @pl.when(jnp.logical_not(own))
        def _(n=n, to_pair=to_pair, to_red=to_red):
            pltpu.make_async_remote_copy(
                src_ref=sendbuf.at[n], dst_ref=recvbuf.at[red],
                send_sem=part_send.at[n], recv_sem=part_recv.at[red],
                device_id=(to_pair, to_red), device_id_type=MESH,
            ).wait_send()


def shards(three_center, occ_src, occ_block, occ_blocks, virt_block, virt_blocks):
    naux, ntiles, area = three_center.shape
    tiles = three_center.reshape(naux, ntiles * area)
    mix = mixing_matrix(occ_src, occ_block, occ_blocks)
    me = lax.axis_index("pair")
    listed = lax.dynamic_index_in_dim(virt_block[0, :, 0], me, keepdims=False) - 2 * me
    held = virt_blocks[0]
    block = jnp.where(listed == 0, held[0], held[1]).reshape(BLK, BLK)
    virt = jnp.tile(block, (1, BLK))
    dma = pltpu.SemaphoreType.DMA
    bf16 = jnp.bfloat16
    return pl.pallas_call(
        kernel,
        out_shape=jax.ShapeDtypeStruct((naux, naux), jnp.float32),
        in_specs=[
            pl.BlockSpec(memory_space=pl.ANY),
            pl.BlockSpec(memory_space=pltpu.VMEM),
            pl.BlockSpec(memory_space=pltpu.VMEM),
        ],
        out_specs=pl.BlockSpec(memory_space=pltpu.VMEM),
        scratch_shapes=[
            pltpu.VMEM((8 * naux, ntiles * area), bf16),
            pltpu.VMEM((ntiles, ntiles * area, area), bf16),
            pltpu.VMEM((area, area), jnp.float32),
            pltpu.VMEM((ntiles, area, area), bf16),
            pltpu.VMEM((ntiles, BLK, area), bf16),
            pltpu.VMEM((3 * naux, ntiles * area), bf16),
            pltpu.VMEM((16, naux, naux), bf16),
            pltpu.VMEM((16, naux, naux), bf16),
            dma((CHUNKS,)), dma((CHUNKS,)), dma((CHUNKS,)), dma((CHUNKS,)), dma((1,)), dma((1,)),
            dma((4,)), dma((4,)), dma((16,)), dma((16,)), dma((16,)), dma((16,)), dma((2,)),
        ],
        compiler_params=pltpu.CompilerParams(
            collective_id=0, has_side_effects=True, vmem_limit_bytes=64000000
        ),
    )(tiles, mix, virt)


def solution(mesh):
    placed = (
        P("pair", "red", None),
        P("red", None),
        P("red", None),
        P("red", None),
        P("red", None, None),
        P("red", "pair", None),
    )
    return jax.shard_map(
        shards, mesh=mesh, in_specs=placed, out_specs=P("pair", "red"), check_vma=False
    )
```

```python
import jax
import jax.numpy as jnp
from jax import lax
from jax.experimental import pallas as pl
from jax.experimental.pallas import tpu as pltpu
from jax.sharding import PartitionSpec as P

BLK = 16
MESH = pl.DeviceIdType.MESH
CHUNKS = 3
OFFSETS = (0, -1, 2, 3, 0, 1, -2, -3)
PAIRS = (
    (0, 0), (4, 0),
    (2, 0), (6, 0), (0, 2), (6, 2),
    (3, 0), (7, 0), (3, 2), (7, 2), (7, 3),
    (1, 0), (5, 0), (1, 2), (5, 2), (1, 3),
)


def kernel(
    tiles_hbm, src_ref, block_ref, occ_ref, listed_ref, virt_ref, out_ref,
    rows, wide, xs, mix, kv, virt, kern, sendbuf, recvbuf, summed, arrived,
    far_send, far_recv, fwd_send, fwd_recv, near_send, near_recv, near_sib_send, near_sib_recv,
    sib_send, sib_recv, virt_send, virt_recv, part_send, part_recv, local_sem, final_sem,
):
    naux = tiles_hbm.shape[0]
    ntiles = 16
    area = 256
    step_rows = naux // CHUNKS
    me = lax.axis_index("pair")
    red = lax.axis_index("red")
    z, core = me // 2, me % 2
    sign = 1 - 2 * core

    def at(offset, which):
        return ((z + sign * offset + 16) % 8) * 2 + which

    row_off, row_core, col_off = 0, core, 0
    for n, (row_slot, col_slot) in enumerate(PAIRS):
        here = red == n
        row_off = jnp.where(here, OFFSETS[row_slot], row_off)
        row_core = jnp.where(here, core if row_slot < 4 else 1 - core, row_core)
        col_off = jnp.where(here, OFFSETS[col_slot], col_off)
    to_pair, to_red = at(row_off, row_core), at(col_off, core)

    col_z, col_core = red // 2, red % 2
    col_sign = 1 - 2 * col_core
    delta = (col_sign * (z - col_z) + 16) % 8
    other = (core + col_core) % 2
    maker, adder = me, red
    for n, (row_slot, col_slot) in enumerate(PAIRS):
        here = (delta == (OFFSETS[row_slot] - OFFSETS[col_slot]) % 8) & (other == row_slot // 4)
        maker = jnp.where(here, ((col_z - col_sign * OFFSETS[col_slot] + 16) % 8) * 2 + col_core, maker)
        adder = jnp.where(here, n, adder)

    barrier = pltpu.get_barrier_semaphore()

    def greet(o, c):
        pl.semaphore_signal(barrier, inc=1, device_id=((me + o) % 16, red), device_id_type=MESH)
        return c

    lax.fori_loop(1, 16, greet, 0)

    def greet_plane(o, c):
        pl.semaphore_signal(barrier, inc=1, device_id=(me, (red + o) % 16), device_id_type=MESH)
        return c

    lax.fori_loop(1, 16, greet_plane, 0)
    stays = (maker == me) & (adder == red)

    @pl.when(jnp.logical_not(stays))
    def _():
        pl.semaphore_signal(barrier, inc=1, device_id=(maker, adder), device_id_type=MESH)

    pl.semaphore_wait(barrier, 31 - jnp.where(stays, 1, 0))

    def slot(i):
        return rows.at[pl.ds(i * naux, naux), :]

    def piece(i, c):
        return rows.at[pl.ds(i * naux + c * step_rows, step_rows), :]

    far = []
    for c in range(CHUNKS):
        copy = pltpu.make_async_remote_copy(
            src_ref=tiles_hbm.at[pl.ds(c * step_rows, step_rows), :], dst_ref=piece(2, c),
            send_sem=far_send.at[c], recv_sem=far_recv.at[c],
            device_id=(at(-2, core), red), device_id_type=MESH,
        )
        copy.start()
        far.append(copy)
    own_copy = pltpu.make_async_copy(tiles_hbm, slot(0), local_sem.at[0])
    own_copy.start()
    own_virt = pltpu.make_async_copy(virt_ref.at[0], virt.at[me], local_sem.at[1])
    own_virt.start()

    def virt_copy(o):
        return pltpu.make_async_remote_copy(
            src_ref=virt_ref.at[0], dst_ref=virt.at[me],
            send_sem=virt_send.at[o], recv_sem=virt_recv.at[me],
            device_id=((me + o) % 16, red), device_id_type=MESH,
        )

    def virt_start(o, c):
        virt_copy(o).start()
        return c

    lax.fori_loop(1, 16, virt_start, 0)

    def sibling(i, src):
        return pltpu.make_async_remote_copy(
            src_ref=src, dst_ref=slot(4 + i),
            send_sem=sib_send.at[i], recv_sem=sib_recv.at[i],
            device_id=(z * 2 + 1 - core, red), device_id_type=MESH,
        )

    sib = {0: sibling(0, tiles_hbm), 2: sibling(2, slot(2)), 3: sibling(3, slot(3))}
    sib[0].start()
    near, near_sib = [], []
    for c in range(CHUNKS):
        near.append(pltpu.make_async_remote_copy(
            src_ref=tiles_hbm.at[pl.ds(c * step_rows, step_rows), :], dst_ref=piece(1, c),
            send_sem=near_send.at[c], recv_sem=near_recv.at[c],
            device_id=(at(1, core), red), device_id_type=MESH,
        ))
        near_sib.append(pltpu.make_async_remote_copy(
            src_ref=piece(1, c), dst_ref=piece(5, c),
            send_sem=near_sib_send.at[c], recv_sem=near_sib_recv.at[c],
            device_id=(z * 2 + 1 - core, red), device_id_type=MESH,
        ))
    fwd = [
        pltpu.make_async_remote_copy(
            src_ref=piece(2, c), dst_ref=piece(3, c),
            send_sem=fwd_send.at[c], recv_sem=fwd_recv.at[c],
            device_id=(at(-1, core), red), device_id_type=MESH,
        )
        for c in range(CHUNKS)
    ]

    lane = lax.broadcasted_iota(jnp.int32, (BLK, area), 1)
    sub = lax.broadcasted_iota(jnp.int32, (BLK, area), 0)
    keep = (lane % BLK) == sub
    grow = lax.broadcasted_iota(jnp.int32, (area, area), 0)
    glane = lax.broadcasted_iota(jnp.int32, (area, area), 1)

    same_group = (grow // BLK) == (glane // BLK)
    same_place = (grow % BLK) == (glane % BLK)
    across = same_group.astype(jnp.float32).astype(jnp.bfloat16)
    along = same_place.astype(jnp.float32).astype(jnp.bfloat16)
    trow = lax.broadcasted_iota(jnp.int32, (area, BLK), 0)
    tlane = lax.broadcasted_iota(jnp.int32, (area, BLK), 1)
    repeat = (trow // BLK == tlane).astype(jnp.float32).astype(jnp.bfloat16)
    place = (trow % BLK) == tlane

    def taller(x):
        return jnp.dot(repeat, x, preferred_element_type=jnp.float32)

    fed = taller(src_ref[...].astype(jnp.float32).astype(jnp.bfloat16))
    fed_hot = (fed == (trow % BLK).astype(jnp.float32)).astype(jnp.float32).astype(jnp.bfloat16)
    lanes_of = (lane % BLK == sub).astype(jnp.float32).astype(jnp.bfloat16)
    fed_wide = jnp.where(same_group, jnp.dot(fed_hot, lanes_of, preferred_element_type=jnp.float32), 0.0)
    used = taller(block_ref[...].astype(jnp.float32).astype(jnp.bfloat16))
    used = jnp.sum(jnp.where(place, used, 0.0), axis=1, keepdims=True)
    nblocks = occ_ref.shape[0]
    number = lax.broadcasted_iota(jnp.int32, (area, nblocks), 1).astype(jnp.float32)
    used_hot = (used == number).astype(jnp.float32).astype(jnp.bfloat16)
    picked = jnp.dot(used_hot, occ_ref[...], preferred_element_type=jnp.float32).astype(jnp.bfloat16)
    mix[...] = jnp.dot(
        fed_wide.astype(jnp.bfloat16), picked, preferred_element_type=jnp.float32
    ).astype(jnp.bfloat16)

    def widen(t, c):
        tall = taller(mix[pl.ds(pl.multiple_of(t * BLK, BLK), BLK), :])
        tall = jnp.where(same_place, tall, 0.0).astype(jnp.bfloat16)
        xs[...] = jnp.dot(tall, across, preferred_element_type=jnp.float32)

        def group(q, c2):
            base = q * 16
            for r in range(16):
                row = xs[pl.ds(base + r, 1), :]
                value = jnp.where(keep, jnp.broadcast_to(row, (BLK, area)), 0.0)
                wide[t, pl.ds(pl.multiple_of((base + r) * BLK, BLK), BLK), :] = value.astype(jnp.bfloat16)
            return c2

        lax.fori_loop(0, area // 16, group, 0)
        return c

    lax.fori_loop(0, ntiles, widen, 0)

    own_virt.wait()

    def virt_wait(o, c):
        src = (me + o) % 16
        pltpu.make_async_remote_copy(
            src_ref=virt_ref.at[0], dst_ref=virt.at[src],
            send_sem=virt_send.at[o], recv_sem=virt_recv.at[src],
            device_id=(src, red), device_id_type=MESH,
        ).wait()
        return c

    lax.fori_loop(1, 16, virt_wait, 0)

    def spread(t, c):
        pair = virt[t].astype(jnp.float32)
        chosen = jnp.where(listed_ref[0, pl.ds(t, 1), :] == 2 * t, pair[0:1, :], pair[1:2, :])
        split = jnp.where(lane // BLK == sub, jnp.broadcast_to(chosen, (BLK, area)), 0.0)
        block = jnp.dot(split.astype(jnp.bfloat16), along, preferred_element_type=jnp.float32)
        tall = jnp.concatenate([block] * BLK, axis=0)
        kv[t] = jnp.where(same_group, tall, 0.0).astype(jnp.bfloat16)
        return c

    lax.fori_loop(0, ntiles, spread, 0)

    def make_kernel(first, count, begin, end):
        def tile(t, c):
            half = jnp.dot(
                rows[first * naux:(first + count) * naux, :], wide[t], preferred_element_type=jnp.float32
            ).astype(jnp.bfloat16)
            value = jnp.dot(half, kv[t], preferred_element_type=jnp.float32).astype(jnp.bfloat16)
            k0 = {0: 0, 2: 1, 3: 2}[first]
            kern[k0 * naux:(k0 + count) * naux, pl.ds(pl.multiple_of(t * area, area), area)] = value
            return c

        lax.fori_loop(begin, end, tile, 0)

    def product(n):
        row_slot, col_slot = PAIRS[n]
        k0 = {0: 0, 2: 1, 3: 2}[col_slot]
        value = lax.dot_general(
            rows[row_slot * naux:(row_slot + 1) * naux, :], kern[k0 * naux:(k0 + 1) * naux, :],
            (((1,), (1,)), ((), ())), preferred_element_type=jnp.float32,
        )
        tail = value[:, 128:]
        sendbuf[n, 0:naux, :] = value[:, 0:128].astype(jnp.bfloat16)
        folded = jnp.concatenate([tail[i * 16:(i + 1) * 16] for i in range(8)], axis=1)
        sendbuf[n, naux:naux + 16, :] = folded.astype(jnp.bfloat16)
        folded = jnp.concatenate([tail[128:144]] * 8, axis=1)
        sendbuf[n, naux + 16:naux + 32, :] = folded.astype(jnp.bfloat16)

    def part(n):
        return pltpu.make_async_remote_copy(
            src_ref=sendbuf.at[n], dst_ref=recvbuf.at[red],
            send_sem=part_send.at[n], recv_sem=part_recv.at[red],
            device_id=(me, n), device_id_type=MESH,
        )

    def flush(begin, count):
        def one(o, c):
            n = begin + (red + o) % count

            @pl.when(n == red)
            def _():
                pltpu.make_async_copy(sendbuf.at[n], recvbuf.at[red], part_recv.at[red]).start()

            @pl.when(n != red)
            def _():
                part(n).start()

            return c

        lax.fori_loop(0, count, one, 0)

    own_copy.wait()

    def relay(c):
        far[c].wait_recv()
        fwd[c].start()

    relay(0)
    make_kernel(0, 1, 0, 8)
    relay(1)
    for c in range(CHUNKS):
        near[c].start()
    make_kernel(0, 1, 8, 16)
    relay(2)
    sib[2].start()
    sib[0].wait_recv()
    product(0)
    product(1)
    make_kernel(2, 1, 0, 16)
    sib[2].wait_recv()
    for n in range(2, 6):
        product(n)
    flush(0, 6)
    for c in range(CHUNKS):
        fwd[c].wait_recv()
    sib[3].start()
    make_kernel(3, 1, 0, 16)
    product(6)
    product(8)
    sib[3].wait_recv()
    for n in (7, 9, 10):
        product(n)
    flush(6, 5)
    for c in range(CHUNKS):
        near[c].wait_recv()
        near_sib[c].start()
    for n in (11, 13, 15):
        product(n)
    for c in range(CHUNKS):
        near_sib[c].wait_recv()
    for n in (12, 14):
        product(n)
    flush(11, 5)

    total = jnp.zeros(summed.shape, jnp.float32)
    for g in range(16):
        pltpu.make_async_copy(sendbuf.at[0], recvbuf.at[g], part_recv.at[g]).wait()
        total = total + recvbuf[g].astype(jnp.float32)
    summed[...] = total
    final = pltpu.make_async_remote_copy(
        src_ref=summed, dst_ref=arrived, send_sem=final_sem.at[0], recv_sem=final_sem.at[1],
        device_id=(to_pair, to_red), device_id_type=MESH,
    )

    @pl.when(stays)
    def _():
        pltpu.make_async_copy(summed, arrived, final_sem.at[1]).start()

    @pl.when(jnp.logical_not(stays))
    def _():
        final.start()

    pltpu.make_async_copy(summed, arrived, final_sem.at[1]).wait()
    out_ref[:, 0:128] = arrived[0:naux, :]
    for i in range(8):
        out_ref[i * 16:(i + 1) * 16, 128:144] = arrived[naux:naux + 16, i * 16:(i + 1) * 16]
    out_ref[128:144, 128:144] = arrived[naux + 16:naux + 32, 0:16]

    @pl.when(jnp.logical_not(stays))
    def _():
        final.wait_send()

    for c in range(CHUNKS):
        far[c].wait_send()
        fwd[c].wait_send()
        near[c].wait_send()
        near_sib[c].wait_send()
    for i in (0, 2, 3):
        sib[i].wait_send()

    def sent(o, c):
        part((red + o) % 16).wait_send()
        return c

    lax.fori_loop(1, 16, sent, 0)


def shards(three_center, occ_src, occ_block, occ_blocks, virt_block, virt_blocks):
    naux, ntiles, area = three_center.shape
    tiles = three_center.reshape(naux, ntiles * area)
    dma = pltpu.SemaphoreType.DMA
    bf16 = jnp.bfloat16
    return pl.pallas_call(
        kernel,
        out_shape=jax.ShapeDtypeStruct((naux, naux), jnp.float32),
        in_specs=[
            pl.BlockSpec(memory_space=pl.ANY),
        ] + [pl.BlockSpec(memory_space=pltpu.VMEM)] * 5,
        out_specs=pl.BlockSpec(memory_space=pltpu.VMEM),
        scratch_shapes=[
            pltpu.VMEM((8 * naux, ntiles * area), bf16),
            pltpu.VMEM((ntiles, ntiles * area, area), bf16),
            pltpu.VMEM((area, area), jnp.float32),
            pltpu.VMEM((area, area), bf16),
            pltpu.VMEM((ntiles, area, area), bf16),
            pltpu.VMEM((ntiles,) + virt_blocks.shape[1:], bf16),
            pltpu.VMEM((3 * naux, ntiles * area), bf16),
            pltpu.VMEM((16, naux + 32, 128), bf16),
            pltpu.VMEM((16, naux + 32, 128), bf16),
            pltpu.VMEM((naux + 32, 128), jnp.float32),
            pltpu.VMEM((naux + 32, 128), jnp.float32),
            dma((CHUNKS,)), dma((CHUNKS,)), dma((CHUNKS,)), dma((CHUNKS,)),
            dma((CHUNKS,)), dma((CHUNKS,)), dma((CHUNKS,)), dma((CHUNKS,)),
            dma((4,)), dma((4,)), dma((16,)), dma((16,)), dma((16,)), dma((16,)), dma((2,)), dma((2,)),
        ],
        compiler_params=pltpu.CompilerParams(
            collective_id=0, has_side_effects=True, vmem_limit_bytes=64000000
        ),
    )(tiles, occ_src, occ_block, occ_blocks, virt_block, virt_blocks)


def solution(mesh):
    placed = (
        P("pair", "red", None),
        P("red", None),
        P("red", None),
        P("red", None),
        P("red", None, None),
        P("red", "pair", None),
    )
    return jax.shard_map(
        shards, mesh=mesh, in_specs=placed, out_specs=P("pair", "red"), check_vma=False
    )
```

```python
import jax
import jax.numpy as jnp
from jax import lax
from jax.experimental import pallas as pl
from jax.experimental.pallas import tpu as pltpu
from jax.sharding import PartitionSpec as P

BLK = 16
MESH = pl.DeviceIdType.MESH
CHUNKS = 3
OFFSETS = (0, -1, 2, 3, 0, 1, -2, -3)
PAIRS = (
    (0, 0), (4, 0),
    (2, 0), (6, 0), (0, 2), (6, 2),
    (3, 0), (7, 0), (3, 2), (7, 2), (7, 3),
    (1, 0), (5, 0), (1, 2), (5, 2), (1, 3),
)


def kernel(
    tiles_hbm, src_ref, block_ref, occ_ref, listed_ref, virt_ref, out_ref,
    rows, wide, xs, mix, kv, virt, kern, sendbuf, recvbuf, summed, arrived,
    far_send, far_recv, fwd_send, fwd_recv, near_send, near_recv, near_sib_send, near_sib_recv,
    sib_send, sib_recv, virt_send, virt_recv, part_send, part_recv, local_sem, final_sem,
):
    naux = tiles_hbm.shape[0]
    ntiles = 16
    area = 256
    step_rows = naux // CHUNKS
    me = lax.axis_index("pair")
    red = lax.axis_index("red")
    z, core = me // 2, me % 2
    sign = 1 - 2 * core

    def at(offset, which):
        return ((z + sign * offset + 16) % 8) * 2 + which

    row_off, row_core, col_off = 0, core, 0
    for n, (row_slot, col_slot) in enumerate(PAIRS):
        here = red == n
        row_off = jnp.where(here, OFFSETS[row_slot], row_off)
        row_core = jnp.where(here, core if row_slot < 4 else 1 - core, row_core)
        col_off = jnp.where(here, OFFSETS[col_slot], col_off)
    to_pair, to_red = at(row_off, row_core), at(col_off, core)

    col_z, col_core = red // 2, red % 2
    col_sign = 1 - 2 * col_core
    delta = (col_sign * (z - col_z) + 16) % 8
    other = (core + col_core) % 2
    maker, adder = me, red
    for n, (row_slot, col_slot) in enumerate(PAIRS):
        here = (delta == (OFFSETS[row_slot] - OFFSETS[col_slot]) % 8) & (other == row_slot // 4)
        maker = jnp.where(here, ((col_z - col_sign * OFFSETS[col_slot] + 16) % 8) * 2 + col_core, maker)
        adder = jnp.where(here, n, adder)

    barrier = pltpu.get_barrier_semaphore()

    def greet(o, c):
        pl.semaphore_signal(barrier, inc=1, device_id=((me + o) % 16, red), device_id_type=MESH)
        return c

    lax.fori_loop(1, 16, greet, 0)

    def greet_plane(o, c):
        pl.semaphore_signal(barrier, inc=1, device_id=(me, (red + o) % 16), device_id_type=MESH)
        return c

    lax.fori_loop(1, 16, greet_plane, 0)
    stays = (maker == me) & (adder == red)

    @pl.when(jnp.logical_not(stays))
    def _():
        pl.semaphore_signal(barrier, inc=1, device_id=(maker, adder), device_id_type=MESH)

    pl.semaphore_wait(barrier, 31 - jnp.where(stays, 1, 0))

    def slot(i):
        return rows.at[pl.ds(i * naux, naux), :]

    def piece(i, c):
        return rows.at[pl.ds(i * naux + c * step_rows, step_rows), :]

    far = []
    for c in range(CHUNKS):
        copy = pltpu.make_async_remote_copy(
            src_ref=tiles_hbm.at[pl.ds(c * step_rows, step_rows), :], dst_ref=piece(2, c),
            send_sem=far_send.at[c], recv_sem=far_recv.at[c],
            device_id=(at(-2, core), red), device_id_type=MESH,
        )
        copy.start()
        far.append(copy)
    own_copy = pltpu.make_async_copy(tiles_hbm, slot(0), local_sem.at[0])
    own_copy.start()
    own_virt = pltpu.make_async_copy(virt_ref.at[0], virt.at[me], local_sem.at[1])
    own_virt.start()

    def virt_copy(o):
        return pltpu.make_async_remote_copy(
            src_ref=virt_ref.at[0], dst_ref=virt.at[me],
            send_sem=virt_send.at[o], recv_sem=virt_recv.at[me],
            device_id=((me + o) % 16, red), device_id_type=MESH,
        )

    def virt_start(o, c):
        virt_copy(o).start()
        return c

    lax.fori_loop(1, 16, virt_start, 0)

    def sibling(i, src):
        return pltpu.make_async_remote_copy(
            src_ref=src, dst_ref=slot(4 + i),
            send_sem=sib_send.at[i], recv_sem=sib_recv.at[i],
            device_id=(z * 2 + 1 - core, red), device_id_type=MESH,
        )

    sib = {0: sibling(0, tiles_hbm), 2: sibling(2, slot(2)), 3: sibling(3, slot(3))}
    sib[0].start()
    near, near_sib = [], []
    for c in range(CHUNKS):
        near.append(pltpu.make_async_remote_copy(
            src_ref=tiles_hbm.at[pl.ds(c * step_rows, step_rows), :], dst_ref=piece(1, c),
            send_sem=near_send.at[c], recv_sem=near_recv.at[c],
            device_id=(at(1, core), red), device_id_type=MESH,
        ))
        near_sib.append(pltpu.make_async_remote_copy(
            src_ref=piece(1, c), dst_ref=piece(5, c),
            send_sem=near_sib_send.at[c], recv_sem=near_sib_recv.at[c],
            device_id=(z * 2 + 1 - core, red), device_id_type=MESH,
        ))
    fwd = [
        pltpu.make_async_remote_copy(
            src_ref=piece(2, c), dst_ref=piece(3, c),
            send_sem=fwd_send.at[c], recv_sem=fwd_recv.at[c],
            device_id=(at(-1, core), red), device_id_type=MESH,
        )
        for c in range(CHUNKS)
    ]

    def relay(c):
        far[c].wait_recv()
        fwd[c].start()

    lane = lax.broadcasted_iota(jnp.int32, (BLK, area), 1)
    sub = lax.broadcasted_iota(jnp.int32, (BLK, area), 0)
    keep = (lane % BLK) == sub
    grow = lax.broadcasted_iota(jnp.int32, (area, area), 0)
    glane = lax.broadcasted_iota(jnp.int32, (area, area), 1)

    same_group = (grow // BLK) == (glane // BLK)
    same_place = (grow % BLK) == (glane % BLK)
    across = same_group.astype(jnp.float32).astype(jnp.bfloat16)
    along = same_place.astype(jnp.float32).astype(jnp.bfloat16)
    trow = lax.broadcasted_iota(jnp.int32, (area, BLK), 0)
    tlane = lax.broadcasted_iota(jnp.int32, (area, BLK), 1)
    repeat = (trow // BLK == tlane).astype(jnp.float32).astype(jnp.bfloat16)
    place = (trow % BLK) == tlane

    def taller(x):
        return jnp.dot(repeat, x, preferred_element_type=jnp.float32)

    fed = taller(src_ref[...].astype(jnp.float32).astype(jnp.bfloat16))
    fed_hot = (fed == (trow % BLK).astype(jnp.float32)).astype(jnp.float32).astype(jnp.bfloat16)
    lanes_of = (lane % BLK == sub).astype(jnp.float32).astype(jnp.bfloat16)
    fed_wide = jnp.where(same_group, jnp.dot(fed_hot, lanes_of, preferred_element_type=jnp.float32), 0.0)
    used = taller(block_ref[...].astype(jnp.float32).astype(jnp.bfloat16))
    used = jnp.sum(jnp.where(place, used, 0.0), axis=1, keepdims=True)
    nblocks = occ_ref.shape[0]
    number = lax.broadcasted_iota(jnp.int32, (area, nblocks), 1).astype(jnp.float32)
    used_hot = (used == number).astype(jnp.float32).astype(jnp.bfloat16)
    picked = jnp.dot(used_hot, occ_ref[...], preferred_element_type=jnp.float32).astype(jnp.bfloat16)
    mix[...] = jnp.dot(
        fed_wide.astype(jnp.bfloat16), picked, preferred_element_type=jnp.float32
    ).astype(jnp.bfloat16)

    def widen(t, c):
        tall = taller(mix[pl.ds(pl.multiple_of(t * BLK, BLK), BLK), :])
        tall = jnp.where(same_place, tall, 0.0).astype(jnp.bfloat16)
        xs[...] = jnp.dot(tall, across, preferred_element_type=jnp.float32)

        def group(q, c2):
            base = q * 16
            for r in range(16):
                row = xs[pl.ds(base + r, 1), :]
                value = jnp.where(keep, jnp.broadcast_to(row, (BLK, area)), 0.0)
                wide[t, pl.ds(pl.multiple_of((base + r) * BLK, BLK), BLK), :] = value.astype(jnp.bfloat16)
            return c2

        lax.fori_loop(0, area // 16, group, 0)
        return c

    lax.fori_loop(0, 11, widen, 0)
    relay(0)
    lax.fori_loop(11, ntiles, widen, 0)

    own_virt.wait()

    def virt_wait(o, c):
        src = (me + o) % 16
        pltpu.make_async_remote_copy(
            src_ref=virt_ref.at[0], dst_ref=virt.at[src],
            send_sem=virt_send.at[o], recv_sem=virt_recv.at[src],
            device_id=(src, red), device_id_type=MESH,
        ).wait()
        return c

    lax.fori_loop(1, 16, virt_wait, 0)

    def spread(t, c):
        pair = virt[t].astype(jnp.float32)
        chosen = jnp.where(listed_ref[0, pl.ds(t, 1), :] == 2 * t, pair[0:1, :], pair[1:2, :])
        split = jnp.where(lane // BLK == sub, jnp.broadcast_to(chosen, (BLK, area)), 0.0)
        block = jnp.dot(split.astype(jnp.bfloat16), along, preferred_element_type=jnp.float32)
        tall = jnp.concatenate([block] * BLK, axis=0)
        kv[t] = jnp.where(same_group, tall, 0.0).astype(jnp.bfloat16)
        return c

    lax.fori_loop(0, ntiles, spread, 0)

    def make_kernel(first, count, begin, end):
        def tile(t, c):
            half = jnp.dot(
                rows[first * naux:(first + count) * naux, :], wide[t], preferred_element_type=jnp.float32
            ).astype(jnp.bfloat16)
            value = jnp.dot(half, kv[t], preferred_element_type=jnp.float32).astype(jnp.bfloat16)
            k0 = {0: 0, 2: 1, 3: 2}[first]
            kern[k0 * naux:(k0 + count) * naux, pl.ds(pl.multiple_of(t * area, area), area)] = value
            return c

        lax.fori_loop(begin, end, tile, 0)

    def product(n):
        row_slot, col_slot = PAIRS[n]
        k0 = {0: 0, 2: 1, 3: 2}[col_slot]
        value = lax.dot_general(
            rows[row_slot * naux:(row_slot + 1) * naux, :], kern[k0 * naux:(k0 + 1) * naux, :],
            (((1,), (1,)), ((), ())), preferred_element_type=jnp.float32,
        )
        tail = value[:, 128:]
        sendbuf[n, 0:naux, :] = value[:, 0:128].astype(jnp.bfloat16)
        folded = jnp.concatenate([tail[i * 16:(i + 1) * 16] for i in range(8)], axis=1)
        sendbuf[n, naux:naux + 16, :] = folded.astype(jnp.bfloat16)
        folded = jnp.concatenate([tail[128:144]] * 8, axis=1)
        sendbuf[n, naux + 16:naux + 32, :] = folded.astype(jnp.bfloat16)

    def part(n):
        return pltpu.make_async_remote_copy(
            src_ref=sendbuf.at[n], dst_ref=recvbuf.at[red],
            send_sem=part_send.at[n], recv_sem=part_recv.at[red],
            device_id=(me, n), device_id_type=MESH,
        )

    def flush(begin, count):
        def one(o, c):
            n = begin + (red + o) % count

            @pl.when(n == red)
            def _():
                pltpu.make_async_copy(sendbuf.at[n], recvbuf.at[red], part_recv.at[red]).start()

            @pl.when(n != red)
            def _():
                part(n).start()

            return c

        lax.fori_loop(0, count, one, 0)

    own_copy.wait()

    make_kernel(0, 1, 0, 8)
    relay(1)
    make_kernel(0, 1, 8, 16)
    relay(2)
    for c in range(CHUNKS):
        near[c].start()
    sib[2].start()
    sib[0].wait_recv()
    product(0)
    product(1)
    make_kernel(2, 1, 0, 16)
    sib[2].wait_recv()
    for n in range(2, 6):
        product(n)
    flush(0, 6)
    for c in range(CHUNKS):
        fwd[c].wait_recv()
    sib[3].start()
    make_kernel(3, 1, 0, 16)
    product(6)
    product(8)
    sib[3].wait_recv()
    for n in (7, 9, 10):
        product(n)
    flush(6, 5)
    for c in range(CHUNKS):
        near[c].wait_recv()
        near_sib[c].start()
    for n in (11, 13, 15):
        product(n)
    for c in range(CHUNKS):
        near_sib[c].wait_recv()
    for n in (12, 14):
        product(n)
    flush(11, 5)

    total = jnp.zeros(summed.shape, jnp.float32)
    for g in range(16):
        pltpu.make_async_copy(sendbuf.at[0], recvbuf.at[g], part_recv.at[g]).wait()
        total = total + recvbuf[g].astype(jnp.float32)
    summed[...] = total
    final = pltpu.make_async_remote_copy(
        src_ref=summed, dst_ref=arrived, send_sem=final_sem.at[0], recv_sem=final_sem.at[1],
        device_id=(to_pair, to_red), device_id_type=MESH,
    )

    @pl.when(stays)
    def _():
        pltpu.make_async_copy(summed, arrived, final_sem.at[1]).start()

    @pl.when(jnp.logical_not(stays))
    def _():
        final.start()

    pltpu.make_async_copy(summed, arrived, final_sem.at[1]).wait()
    out_ref[:, 0:128] = arrived[0:naux, :]
    for i in range(8):
        out_ref[i * 16:(i + 1) * 16, 128:144] = arrived[naux:naux + 16, i * 16:(i + 1) * 16]
    out_ref[128:144, 128:144] = arrived[naux + 16:naux + 32, 0:16]

    @pl.when(jnp.logical_not(stays))
    def _():
        final.wait_send()

    for c in range(CHUNKS):
        far[c].wait_send()
        fwd[c].wait_send()
        near[c].wait_send()
        near_sib[c].wait_send()
    for i in (0, 2, 3):
        sib[i].wait_send()

    def sent(o, c):
        part((red + o) % 16).wait_send()
        return c

    lax.fori_loop(1, 16, sent, 0)


def shards(three_center, occ_src, occ_block, occ_blocks, virt_block, virt_blocks):
    naux, ntiles, area = three_center.shape
    tiles = three_center.reshape(naux, ntiles * area)
    dma = pltpu.SemaphoreType.DMA
    bf16 = jnp.bfloat16
    return pl.pallas_call(
        kernel,
        out_shape=jax.ShapeDtypeStruct((naux, naux), jnp.float32),
        in_specs=[
            pl.BlockSpec(memory_space=pl.ANY),
        ] + [pl.BlockSpec(memory_space=pltpu.VMEM)] * 5,
        out_specs=pl.BlockSpec(memory_space=pltpu.VMEM),
        scratch_shapes=[
            pltpu.VMEM((8 * naux, ntiles * area), bf16),
            pltpu.VMEM((ntiles, ntiles * area, area), bf16),
            pltpu.VMEM((area, area), jnp.float32),
            pltpu.VMEM((area, area), bf16),
            pltpu.VMEM((ntiles, area, area), bf16),
            pltpu.VMEM((ntiles,) + virt_blocks.shape[1:], bf16),
            pltpu.VMEM((3 * naux, ntiles * area), bf16),
            pltpu.VMEM((16, naux + 32, 128), bf16),
            pltpu.VMEM((16, naux + 32, 128), bf16),
            pltpu.VMEM((naux + 32, 128), jnp.float32),
            pltpu.VMEM((naux + 32, 128), jnp.float32),
            dma((CHUNKS,)), dma((CHUNKS,)), dma((CHUNKS,)), dma((CHUNKS,)),
            dma((CHUNKS,)), dma((CHUNKS,)), dma((CHUNKS,)), dma((CHUNKS,)),
            dma((4,)), dma((4,)), dma((16,)), dma((16,)), dma((16,)), dma((16,)), dma((2,)), dma((2,)),
        ],
        compiler_params=pltpu.CompilerParams(
            collective_id=0, has_side_effects=True, vmem_limit_bytes=64000000
        ),
    )(tiles, occ_src, occ_block, occ_blocks, virt_block, virt_blocks)


def solution(mesh):
    placed = (
        P("pair", "red", None),
        P("red", None),
        P("red", None),
        P("red", None),
        P("red", None, None),
        P("red", "pair", None),
    )
    return jax.shard_map(
        shards, mesh=mesh, in_specs=placed, out_specs=P("pair", "red"), check_vma=False
    )
```
